32 devices in a mesh: tm: 4 (over y, x), vox: 8 (over z, core).
Axes of the slice: x: 2, y: 2, z: 4, core: 2. Of those that a mesh axis runs over, the one named last changes fastest.
Arguments:
- u_train: bfloat16 [3072, 4096], P('tm'), may hold values from -0.109375 to 0.109375
- y_train: bfloat16 [3072, 3072], P('tm', 'vox'), may hold values from -6 to 6
- sing: float32 [4096], replicated, may hold values from 0.5 to 8
- lambdas: float32 [20], replicated, may hold values from 0.1 to 100
- lam_index: int32 [24], P('vox'), may hold values from 0 to 19
- live: int32 [24], P('vox'), may hold values from 0 to 1, as said below
- v_basis: bfloat16 [4096, 4096], P('tm', 'vox'), may hold values from -0.09375 to 0.09375
- x_test: bfloat16 [1024, 4096], P(None, 'tm'), may hold values from -0.09375 to 0.09375
Outputs:
- weights: bfloat16 [4096, 3072], P('tm', 'vox')
- predictions: bfloat16 [1024, 3072], P('tm', 'vox')
The draws below stay inside these ranges and needn't reach their ends.
Inputs may be any that keep to these rules, and one draw needn't show every extreme that they name: Of the 3 voxel blocks that one device along vox holds, at most 2 are live, and some device holds exactly 2.
All inputs are finite; a program needn't handle non-finite values.
Results may differ from the reference program's by a relative error of at most 0.0058.
Values may be sent and summed in bfloat16 or wider, within the bound.
A program may use at most 128 MiB of HBM per device.

```python
import math
import jax
import jax.numpy as jnp

F = 4096
NLAM = 20
BLK = 128
VD = 384
TEST = 1024
TR = 3072
VOX = 3072
NBLK = 24


def draw_live(key, part):
    block_count = VD // BLK
    device_count = NBLK // block_count
    capacity = block_count - block_count // 3
    first_key = jax.random.fold_in(key, 11)
    second_key = jax.random.fold_in(key, 12)
    third_key = jax.random.fold_in(key, 13)
    counts = jax.random.randint(first_key, (device_count,), 1, capacity + 1)
    fullest = jax.random.randint(second_key, (), 0, device_count)
    counts = jnp.where(jnp.arange(device_count) == fullest, capacity, counts)
    scores = jax.random.randint(third_key, (device_count, block_count), 0, 1 << 20)
    scores = scores * block_count + jnp.arange(block_count)[None, :]
    ranking = jnp.argsort(jnp.argsort(scores, axis=1), axis=1)
    marked = (ranking < counts[:, None]).astype(jnp.int32)
    return marked.reshape(NBLK)


def plant(values, rng, least, top_value):
    extent = values.shape
    place = [jax.random.randint(jax.random.fold_in(rng, axis), (), 0, extent[axis]) for axis in range(len(extent))]
    values = values.at[tuple(place)].set(least)
    longest = extent.index(max(extent))
    place[longest] = (place[longest] + 1) % extent[longest]
    return values.at[tuple(place)].set(top_value)


def block_levels(key, extent, cuts, low, top_value):
    gain = 1.0
    for position, shards_of in cuts:
        steps = jax.random.uniform(jax.random.fold_in(jax.random.fold_in(key, 6), position), (shards_of,), jnp.float32, low / len(cuts), top_value / len(cuts))
        gain = gain * jnp.repeat(jnp.exp(steps), extent[position] // shards_of).reshape((-1,) + (1,) * (len(extent) - 1 - position))
    return gain


def centred(stream_key, dims, deviation, bound, cuts=(), kind=jnp.bfloat16):
    result = deviation * jax.random.normal(stream_key, dims, jnp.float32)
    if cuts:
        result = result * block_levels(stream_key, dims, cuts, -0.22, 0.18)
    return jnp.clip(result, -bound, bound).astype(kind)


def setup_inputs(seed: int = 0) -> dict:
    key_list = jax.random.split(jax.random.key(seed), 9)
    u_train = centred(key_list[0], (TR, F), TR ** -0.5, 0.109375, ((0, 4),))
    y_train = centred(key_list[1], (TR, VOX), 1.0, 6.0, ((0, 4), (1, 8)))
    sing = jnp.clip(jnp.exp(jax.random.uniform(key_list[2], (F,), jnp.float32, math.log(0.5), math.log(8.0))), 0.5, 8.0)
    lambdas = jnp.clip(jnp.exp(jax.random.uniform(key_list[3], (NLAM,), jnp.float32, math.log(0.1), math.log(100.0))), 0.1, 100.0)
    lam_index = plant(jax.random.randint(key_list[4], (NBLK,), 0, NLAM), jax.random.fold_in(key_list[4], 1), 0, NLAM - 1).astype(jnp.int32)
    live = draw_live(jax.random.fold_in(key_list[8], 71), 0)
    v_basis = centred(key_list[6], (F, F), F ** -0.5, 0.09375, ((0, 4), (1, 8)))
    x_test = centred(key_list[7], (TEST, F), F ** -0.5, 0.09375, ((1, 4),))
    return dict(u_train=u_train, y_train=y_train, sing=sing, lambdas=lambdas, lam_index=lam_index, live=live, v_basis=v_basis, x_test=x_test)


def reference(u_train, y_train, sing, lambdas, lam_index, live, v_basis, x_test):
    filters = sing[None, :] / (sing[None, :] * sing[None, :] + lambdas[:, None])
    products = jnp.dot(u_train.T, y_train, preferred_element_type=jnp.float32)
    chosen = filters[lam_index] * live[:, None].astype(jnp.float32)
    blocks = products.reshape(F, NBLK, BLK) * chosen.T[:, :, None]
    filtered = blocks.reshape(F, VOX).astype(jnp.bfloat16)
    weights = jnp.dot(v_basis, filtered, preferred_element_type=jnp.float32).astype(jnp.bfloat16)
    predictions = jnp.dot(x_test, weights, preferred_element_type=jnp.float32).astype(jnp.bfloat16)
    return weights, predictions
```

```python
import functools

import jax
import jax.numpy as jnp
from jax import lax
from jax.experimental import pallas as pl
from jax.experimental.pallas import tpu as pltpu
from jax.sharding import PartitionSpec as P

BLK = 128
CHUNKS = 4
TILE = 256
MESH = pl.DeviceIdType.MESH


def kernel(
    n_t,
    n_v,
    cap,
    live_ref,
    index_ref,
    lambda_ref,
    sing_ref,
    y_ref,
    u_ref,
    v_ref,
    x_ref,
    w_ref,
    pred_ref,
    u_buf,
    x_buf,
    v_all,
    part_out,
    part_in,
    part_own,
    filt,
    acc,
    pred_acc,
    pred_out,
    pred_in,
    u_sem,
    x_sem,
    own_sem,
    right_sem,
    left_sem,
    line_sem,
    pair_send,
    pair_recv,
    rs_send,
    rs_recv,
    ag_send,
    ag_recv,
    q_send,
    q_recv,
):
    t = lax.axis_index("tm")
    v = lax.axis_index("vox")
    n_z = n_v // 2
    z, core = v // 2, v % 2
    mate = z * 2 + 1 - core
    rows_v, depth = v_ref.shape
    blocks = live_ref.shape[0]
    share = part_own.shape[1]
    test_rows = pred_out.shape[1]
    rc = rows_v // CHUNKS

    def u_copy(owner):
        cols = pl.ds(pl.multiple_of(owner * share, share), share)
        return pltpu.make_async_copy(u_ref.at[:, cols], u_buf.at[:, cols], u_sem.at[owner])

    def own_copy(ch):
        rows = pl.ds(ch * rc, rc)
        return pltpu.make_async_copy(v_ref.at[rows], v_all.at[v, rows], own_sem.at[ch])

    def line_copy(src, ch, step, first=False):
        rows = pl.ds(ch * rc, rc)
        slot = src * 2 + core
        return pltpu.make_async_remote_copy(
            src_ref=v_ref.at[rows] if first else v_all.at[slot, rows],
            dst_ref=v_all.at[slot, rows],
            send_sem=(right_sem if step > 0 else left_sem).at[src, ch],
            recv_sem=line_sem.at[src, ch],
            device_id={"vox": v + 2 * step},
            device_id_type=MESH,
        )

    def pair_copy(src, ch, first=False):
        rows = pl.ds(ch * rc, rc)
        slot = src * 2 + core
        return pltpu.make_async_remote_copy(
            src_ref=v_ref.at[rows] if first else v_all.at[slot, rows],
            dst_ref=v_all.at[slot, rows],
            send_sem=pair_send.at[src, ch],
            recv_sem=pair_recv.at[src, ch],
            device_id={"vox": mate},
            device_id_type=MESH,
        )

    def pair_arrival(src, ch):
        rows = pl.ds(ch * rc, rc)
        slot = src * 2 + 1 - core
        return pltpu.make_async_remote_copy(
            src_ref=v_all.at[slot, rows],
            dst_ref=v_all.at[slot, rows],
            send_sem=pair_send.at[src, ch],
            recv_sem=pair_recv.at[src, ch],
            device_id={"vox": mate},
            device_id_type=MESH,
        )

    def peer(d):
        return lax.rem(t + d, n_t)

    def part_copy(to, owner):
        return pltpu.make_async_remote_copy(
            src_ref=part_out.at[to],
            dst_ref=part_in.at[owner],
            send_sem=rs_send.at[to],
            recv_sem=rs_recv.at[owner],
            device_id={"tm": to},
            device_id_type=MESH,
        )

    def filt_copy(to, owner):
        return pltpu.make_async_remote_copy(
            src_ref=filt.at[owner],
            dst_ref=filt.at[owner],
            send_sem=ag_send.at[to],
            recv_sem=ag_recv.at[owner],
            device_id={"tm": to},
            device_id_type=MESH,
        )

    def pred_copy(to, owner):
        return pltpu.make_async_remote_copy(
            src_ref=pred_out.at[to],
            dst_ref=pred_in.at[owner],
            send_sem=q_send.at[to],
            recv_sem=q_recv.at[owner],
            device_id={"tm": to},
            device_id_type=MESH,
        )

    for d in range(n_t):
        u_copy(peer((d + 1) % n_t)).start()

    barrier = pltpu.get_barrier_semaphore()
    for d in range(1, n_t):
        pl.semaphore_signal(barrier, inc=1, device_id={"tm": peer(d)}, device_id_type=MESH)
    pl.semaphore_signal(barrier, inc=1, device_id={"vox": mate}, device_id_type=MESH)

    @pl.when(z > 0)
    def _():
        pl.semaphore_signal(barrier, inc=1, device_id={"vox": v - 2}, device_id_type=MESH)

    @pl.when(z < n_z - 1)
    def _():
        pl.semaphore_signal(barrier, inc=1, device_id={"vox": v + 2}, device_id_type=MESH)

    neighbours = jnp.where(z > 0, 1, 0) + jnp.where(z < n_z - 1, 1, 0)
    pl.semaphore_wait(barrier, n_t + neighbours)

    for ch in range(CHUNKS):

        @pl.when(z > 0)
        def _():
            line_copy(z, ch, -1, True).start()

        @pl.when(z < n_z - 1)
        def _():
            line_copy(z, ch, 1, True).start()

    live = [live_ref[i] for i in range(blocks)]
    before = [sum(live[:i], jnp.int32(0)) for i in range(blocks)]
    pick = [
        [jnp.where(before[i] == j, live[i], 0).astype(jnp.float32) for i in range(blocks)]
        for j in range(cap)
    ]
    lam = [lambda_ref[index_ref[i]] for i in range(blocks)]
    slot_lam = [sum(pick[j][i] * lam[i] for i in range(blocks)) for j in range(cap)]
    slot_live = [sum(pick[j][i] for i in range(blocks)) for j in range(cap)]

    y_cols = [y_ref[:, i * BLK : (i + 1) * BLK].astype(jnp.float32) for i in range(blocks)]
    y_t = jnp.concatenate(
        [sum(pick[j][i] * y_cols[i] for i in range(blocks)).T for j in range(cap)], axis=0
    ).astype(jnp.bfloat16)

    for d in range(1, n_t + 1):
        to = peer(d % n_t)
        u_copy(to).wait()

        def tile(i, _, to=to, d=d):
            off = pl.multiple_of(i * TILE, TILE)
            cols = pl.ds(pl.multiple_of(to * share + i * TILE, TILE), TILE)
            value = jnp.dot(y_t, u_buf[:, cols], preferred_element_type=jnp.float32)
            if d < n_t:
                part_out[to, :, pl.ds(off, TILE)] = value.astype(jnp.bfloat16)
            else:
                part_own[:, pl.ds(off, TILE)] = value
            return 0

        lax.fori_loop(0, share // TILE, tile, 0)
        if d < n_t:
            part_copy(to, t).start()

    for ch in range(CHUNKS):
        pair_copy(z, ch, True).start()
        own_copy(ch).start()
    x_copy = pltpu.make_async_copy(x_ref, x_buf, x_sem)
    x_copy.start()

    def relay(s, ch):
        low, high = z - 1 - s, z + 1 + s

        @pl.when(low >= 0)
        def _():
            line_copy(low, ch, -1).wait_recv()

            @pl.when(z < n_z - 1)
            def _():
                line_copy(low, ch, 1).start()

            pair_copy(low, ch).start()

        @pl.when(high < n_z)
        def _():
            line_copy(high, ch, 1).wait_recv()

            @pl.when(z > 0)
            def _():
                line_copy(high, ch, -1).start()

            pair_copy(high, ch).start()

    for ch in range(CHUNKS // 2):
        relay(0, ch)

    for d in range(1, n_t):
        part_copy(peer(d), peer(d)).wait_recv()
    for i in range(share // TILE):
        cols = slice(i * TILE, (i + 1) * TILE)
        sing = sing_ref[:, pl.ds(pl.multiple_of(t * share + i * TILE, TILE), TILE)]
        for j in range(cap):
            rows = slice(j * BLK, (j + 1) * BLK)
            total = part_own[rows, cols]
            for d in range(1, n_t):
                total = total + part_in[peer(d), rows, cols].astype(jnp.float32)
            factor = sing / (sing * sing + slot_lam[j]) * slot_live[j]
            filt[t, rows, cols] = (total * factor).astype(jnp.bfloat16)
    for d in range(1, n_t):
        filt_copy(peer(d), t).start()

    for ch in range(CHUNKS // 2, CHUNKS):
        relay(0, ch)

    def relay_step(s, _):
        for ch in range(CHUNKS):
            relay(s, ch)
        return 0

    lax.fori_loop(1, n_z - 2, relay_step, 0)

    for d in range(1, n_t):
        filt_copy(peer(d), peer(d)).wait_recv()

    def term(src, ch):
        pair_arrival(src, ch).wait_recv()
        rows = pl.ds(ch * rc, rc)
        value = None
        for c in range(2):
            slot = src * 2 + c
            start = slot * depth
            owner = start // share
            offset = pl.multiple_of(start - owner * share, depth)
            part = lax.dot_general(
                v_all[slot, rows, :],
                filt[owner, :, pl.ds(offset, depth)],
                (((1,), (1,)), ((), ())),
                preferred_element_type=jnp.float32,
            )
            value = part if value is None else value + part
        return value

    for ch in range(CHUNKS):
        own_copy(ch).wait()
        acc[pl.ds(ch * rc, rc), :] = term(z, ch)

    def add_step(s, _):
        low, high = z - 1 - s, z + 1 + s
        for ch in range(CHUNKS):
            rows = pl.ds(ch * rc, rc)

            @pl.when(low >= 0)
            def _():
                acc[rows, :] += term(low, ch)

            @pl.when(high < n_z)
            def _():
                acc[rows, :] += term(high, ch)

        return 0

    lax.fori_loop(0, n_z - 2, add_step, 0)
    x_copy.wait()

    def expand(values):
        return [
            sum(pick[j][i] * values[:, j * BLK : (j + 1) * BLK] for j in range(cap))
            for i in range(blocks)
        ]

    def finish(ch):
        rows = slice(ch * rc, (ch + 1) * rc)

        @pl.when(z == 0)
        def _():
            acc[rows, :] += term(n_z - 1, ch)

        @pl.when(z == n_z - 1)
        def _():
            acc[rows, :] += term(0, ch)

        weights = acc[rows, :].astype(jnp.bfloat16)
        for i, block in enumerate(expand(weights.astype(jnp.float32))):
            w_ref[rows, i * BLK : (i + 1) * BLK] = block.astype(jnp.bfloat16)
        value = jnp.dot(x_buf[:, rows], weights, preferred_element_type=jnp.float32)
        if ch == 0:
            pred_acc[...] = value
        else:
            pred_acc[...] += value

    for ch in range(CHUNKS):
        relay(n_z - 2, ch)
        if ch > 0:
            finish(ch - 1)
    finish(CHUNKS - 1)

    for d in range(1, n_t):
        to = peer(d)
        mine = pl.ds(pl.multiple_of(to * test_rows, test_rows), test_rows)
        pred_out[to] = pred_acc[mine, :].astype(jnp.bfloat16)
        pred_copy(to, t).start()
    for d in range(1, n_t):
        pred_copy(peer(d), peer(d)).wait_recv()
    total = pred_acc[pl.ds(pl.multiple_of(t * test_rows, test_rows), test_rows), :]
    for d in range(1, n_t):
        total = total + pred_in[peer(d)].astype(jnp.float32)
    for i, block in enumerate(expand(total)):
        pred_ref[:, i * BLK : (i + 1) * BLK] = block.astype(jnp.bfloat16)

    for d in range(1, n_t):
        part_copy(peer(d), t).wait_send()
        filt_copy(peer(d), t).wait_send()
        pred_copy(peer(d), t).wait_send()

    def drain(src, _):
        for ch in range(CHUNKS):
            pair_copy(src, ch).wait_send()

            @pl.when((src <= z) & (z < n_z - 1))
            def _():
                line_copy(src, ch, 1).wait_send()

            @pl.when((src >= z) & (z > 0))
            def _():
                line_copy(src, ch, -1).wait_send()

        return 0

    lax.fori_loop(0, n_z, drain, 0)


def body(n_t, n_v, u_train, y_train, sing, lambdas, lam_index, live, v_basis, x_test):
    time_rows, features = u_train.shape
    columns = y_train.shape[1]
    blocks = lam_index.shape[0]
    cap = blocks - blocks // 3
    used = cap * BLK
    rows_v, depth = v_basis.shape
    tests = x_test.shape[0]
    share = features // n_t
    n_z = n_v // 2
    low, full = jnp.bfloat16, jnp.float32
    smem = pl.BlockSpec(memory_space=pltpu.SMEM)
    vmem = pl.BlockSpec(memory_space=pltpu.VMEM)
    anywhere = pl.BlockSpec(memory_space=pl.ANY)
    dma = pltpu.SemaphoreType.DMA
    return pl.pallas_call(
        functools.partial(kernel, n_t, n_v, cap),
        out_shape=(
            jax.ShapeDtypeStruct((rows_v, columns), low),
            jax.ShapeDtypeStruct((tests // n_t, columns), low),
        ),
        in_specs=[smem, smem, smem, vmem, vmem, anywhere, anywhere, anywhere],
        out_specs=(vmem, vmem),
        scratch_shapes=[
            pltpu.VMEM((time_rows, features), low),
            pltpu.VMEM((tests, rows_v), low),
            pltpu.VMEM((n_v, rows_v, depth), low),
            pltpu.VMEM((n_t, used, share), low),
            pltpu.VMEM((n_t, used, share), low),
            pltpu.VMEM((used, share), full),
            pltpu.VMEM((n_t, used, share), low),
            pltpu.VMEM((rows_v, used), full),
            pltpu.VMEM((tests, used), full),
            pltpu.VMEM((n_t, tests // n_t, used), low),
            pltpu.VMEM((n_t, tests // n_t, used), low),
            dma((n_t,)),
            dma,
            dma((CHUNKS,)),
            dma((n_z, CHUNKS)),
            dma((n_z, CHUNKS)),
            dma((n_z, CHUNKS)),
            dma((n_z, CHUNKS)),
            dma((n_z, CHUNKS)),
            dma((n_t,)),
            dma((n_t,)),
            dma((n_t,)),
            dma((n_t,)),
            dma((n_t,)),
            dma((n_t,)),
        ],
        compiler_params=pltpu.CompilerParams(collective_id=0, has_side_effects=True),
    )(live, lam_index, lambdas, sing.reshape(1, features), y_train, u_train, v_basis, x_test)


def solution(mesh):
    placed = (
        P("tm", None),
        P("tm", "vox"),
        P(),
        P(),
        P("vox"),
        P("vox"),
        P("tm", "vox"),
        P(None, "tm"),
    )
    return jax.shard_map(
        functools.partial(body, mesh.shape["tm"], mesh.shape["vox"]),
        mesh=mesh,
        in_specs=placed,
        out_specs=(P("tm", "vox"), P("tm", "vox")),
        check_vma=False,
    )
```

```python
import functools

import jax
import jax.numpy as jnp
from jax import lax
from jax.experimental import pallas as pl
from jax.experimental.pallas import tpu as pltpu
from jax.sharding import PartitionSpec as P

BLK = 128
CHUNKS = 4
TILE = 256
MESH = pl.DeviceIdType.MESH


def kernel(
    n_t,
    n_v,
    cap,
    live_ref,
    index_ref,
    lambda_ref,
    sing_ref,
    y_ref,
    u_ref,
    v_ref,
    x_ref,
    w_ref,
    pred_ref,
    u_buf,
    x_buf,
    v_all,
    part_out,
    part_in,
    part_own,
    filt,
    acc,
    pred_acc,
    pred_out,
    pred_in,
    u_sem,
    x_sem,
    own_sem,
    right_sem,
    left_sem,
    line_sem,
    pair_send,
    pair_recv,
    rs_send,
    rs_recv,
    ag_send,
    ag_recv,
    q_send,
    q_recv,
    far_filt,
    far_out,
    far_in,
    far_filt_send,
    far_filt_recv,
    far_send,
    far_recv,
):
    t = lax.axis_index("tm")
    v = lax.axis_index("vox")
    n_z = n_v // 2
    z, core = v // 2, v % 2
    mate = z * 2 + 1 - core
    rows_v, depth = v_ref.shape
    blocks = live_ref.shape[0]
    share = part_own.shape[2]
    half = n_z // 2
    span = n_t * share
    first_round = jnp.where(z < half, 1, 0)
    at_low, at_high = z == 0, z == n_z - 1
    is_end = at_low | at_high
    is_helper = (z == 1) | (z == n_z - 2)

    def holds(zz, src):
        return jnp.logical_not(
            ((zz == 0) & (src >= half)) | ((zz == n_z - 1) & (src < half))
        )
    test_rows = pred_out.shape[1]
    rc = rows_v // CHUNKS

    def u_copy(r, owner):
        cols = pl.ds(pl.multiple_of(r * span + owner * share, share), share)
        return pltpu.make_async_copy(u_ref.at[:, cols], u_buf.at[:, cols], u_sem.at[r, owner])

    def own_copy(ch):
        rows = pl.ds(ch * rc, rc)
        return pltpu.make_async_copy(v_ref.at[rows], v_all.at[v, rows], own_sem.at[ch])

    def line_copy(src, ch, step, first=False):
        rows = pl.ds(ch * rc, rc)
        slot = src * 2 + core
        return pltpu.make_async_remote_copy(
            src_ref=v_ref.at[rows] if first else v_all.at[slot, rows],
            dst_ref=v_all.at[slot, rows],
            send_sem=(right_sem if step > 0 else left_sem).at[src, ch],
            recv_sem=line_sem.at[src, ch],
            device_id={"vox": v + 2 * step},
            device_id_type=MESH,
        )

    def pair_copy(src, ch, first=False):
        rows = pl.ds(ch * rc, rc)
        slot = src * 2 + core
        return pltpu.make_async_remote_copy(
            src_ref=v_ref.at[rows] if first else v_all.at[slot, rows],
            dst_ref=v_all.at[slot, rows],
            send_sem=pair_send.at[src, ch],
            recv_sem=pair_recv.at[src, ch],
            device_id={"vox": mate},
            device_id_type=MESH,
        )

    def pair_arrival(src, ch):
        rows = pl.ds(ch * rc, rc)
        slot = src * 2 + 1 - core
        return pltpu.make_async_remote_copy(
            src_ref=v_all.at[slot, rows],
            dst_ref=v_all.at[slot, rows],
            send_sem=pair_send.at[src, ch],
            recv_sem=pair_recv.at[src, ch],
            device_id={"vox": mate},
            device_id_type=MESH,
        )

    def peer(d):
        return lax.rem(t + d, n_t)

    def part_copy(r, to, owner):
        return pltpu.make_async_remote_copy(
            src_ref=part_out.at[r, to],
            dst_ref=part_in.at[r, owner],
            send_sem=rs_send.at[r, to],
            recv_sem=rs_recv.at[r, owner],
            device_id={"tm": to},
            device_id_type=MESH,
        )

    def filt_copy(r, to, owner):
        return pltpu.make_async_remote_copy(
            src_ref=filt.at[r, owner],
            dst_ref=filt.at[r, owner],
            send_sem=ag_send.at[r, to],
            recv_sem=ag_recv.at[r, owner],
            device_id={"tm": to},
            device_id_type=MESH,
        )

    def pred_copy(to, owner):
        return pltpu.make_async_remote_copy(
            src_ref=pred_out.at[to],
            dst_ref=pred_in.at[owner],
            send_sem=q_send.at[to],
            recv_sem=q_recv.at[owner],
            device_id={"tm": to},
            device_id_type=MESH,
        )

    inward = jnp.where(z < half, 1, -1)

    def far_filt_copy(j, step):
        rows = pl.ds(j * BLK, BLK)
        return pltpu.make_async_remote_copy(
            src_ref=filt.at[first_round, :, rows, :],
            dst_ref=far_filt.at[:, rows, :],
            send_sem=far_filt_send.at[j],
            recv_sem=far_filt_recv.at[j],
            device_id={"vox": v + 2 * step},
            device_id_type=MESH,
        )

    def far_copy(j, ch, step):
        rows = pl.ds(ch * rc, rc)
        return pltpu.make_async_remote_copy(
            src_ref=far_out.at[j, rows],
            dst_ref=far_in.at[j, rows],
            send_sem=far_send.at[j, ch],
            recv_sem=far_recv.at[j, ch],
            device_id={"vox": v + 2 * step},
            device_id_type=MESH,
        )

    rounds = (first_round, 1 - first_round)
    for r in rounds:
        for d in range(n_t):
            u_copy(r, peer((d + 1) % n_t)).start()

    barrier = pltpu.get_barrier_semaphore()
    for d in range(1, n_t):
        pl.semaphore_signal(barrier, inc=1, device_id={"tm": peer(d)}, device_id_type=MESH)
    pl.semaphore_signal(barrier, inc=1, device_id={"vox": mate}, device_id_type=MESH)

    @pl.when(z > 0)
    def _():
        pl.semaphore_signal(barrier, inc=1, device_id={"vox": v - 2}, device_id_type=MESH)

    @pl.when(z < n_z - 1)
    def _():
        pl.semaphore_signal(barrier, inc=1, device_id={"vox": v + 2}, device_id_type=MESH)

    neighbours = jnp.where(z > 0, 1, 0) + jnp.where(z < n_z - 1, 1, 0)
    pl.semaphore_wait(barrier, n_t + neighbours)

    for ch in range(CHUNKS):

        @pl.when(z > 0)
        def _():
            line_copy(z, ch, -1, True).start()

        @pl.when(z < n_z - 1)
        def _():
            line_copy(z, ch, 1, True).start()

    live = [live_ref[i] for i in range(blocks)]
    before = [sum(live[:i], jnp.int32(0)) for i in range(blocks)]
    pick = [
        [jnp.where(before[i] == j, live[i], 0).astype(jnp.float32) for i in range(blocks)]
        for j in range(cap)
    ]
    lam = [lambda_ref[index_ref[i]] for i in range(blocks)]
    slot_lam = [sum(pick[j][i] * lam[i] for i in range(blocks)) for j in range(cap)]
    slot_live = [sum(pick[j][i] for i in range(blocks)) for j in range(cap)]

    y_cols = [y_ref[:, i * BLK : (i + 1) * BLK].astype(jnp.float32) for i in range(blocks)]
    y_t = jnp.concatenate(
        [sum(pick[j][i] * y_cols[i] for i in range(blocks)).T for j in range(cap)], axis=0
    ).astype(jnp.bfloat16)

    def make_parts(r):
        for d in range(1, n_t + 1):
            to = peer(d % n_t)
            u_copy(r, to).wait()

            def tile(i, _, to=to, d=d):
                off = pl.multiple_of(i * TILE, TILE)
                cols = pl.ds(pl.multiple_of(r * span + to * share + i * TILE, TILE), TILE)
                value = jnp.dot(y_t, u_buf[:, cols], preferred_element_type=jnp.float32)
                if d < n_t:
                    part_out[r, to, :, pl.ds(off, TILE)] = value.astype(jnp.bfloat16)
                else:
                    part_own[r, :, pl.ds(off, TILE)] = value
                return 0

            lax.fori_loop(0, share // TILE, tile, 0)

    def send_parts(r):
        for d in range(1, n_t):
            part_copy(r, peer(d), t).start()

    def filter_parts(r):
        for d in range(1, n_t):
            part_copy(r, peer(d), peer(d)).wait_recv()
        for i in range(share // TILE):
            cols = slice(i * TILE, (i + 1) * TILE)
            place = pl.multiple_of(r * span + t * share + i * TILE, TILE)
            sing = sing_ref[:, pl.ds(place, TILE)]
            for j in range(cap):
                rows = slice(j * BLK, (j + 1) * BLK)
                total = part_own[r, rows, cols]
                for d in range(1, n_t):
                    total = total + part_in[r, peer(d), rows, cols].astype(jnp.float32)
                factor = sing / (sing * sing + slot_lam[j]) * slot_live[j]
                filt[r, t, rows, cols] = (total * factor).astype(jnp.bfloat16)
        for d in range(1, n_t):
            filt_copy(r, peer(d), t).start()

    def await_filt(r):
        for d in range(1, n_t):
            filt_copy(r, peer(d), peer(d)).wait_recv()

    make_parts(rounds[0])
    send_parts(rounds[0])

    for ch in range(CHUNKS):
        pair_copy(z, ch, True).start()
        own_copy(ch).start()
    x_copy = pltpu.make_async_copy(x_ref, x_buf, x_sem)
    x_copy.start()

    make_parts(rounds[1])

    def relay(s, ch):
        low, high = z - 1 - s, z + 1 + s

        @pl.when((low >= 0) & holds(z, low))
        def _():
            line_copy(low, ch, -1).wait_recv()

            @pl.when((z < n_z - 1) & holds(z + 1, low))
            def _():
                line_copy(low, ch, 1).start()

            pair_copy(low, ch).start()

        @pl.when((high < n_z) & holds(z, high))
        def _():
            line_copy(high, ch, 1).wait_recv()

            @pl.when((z > 0) & holds(z - 1, high))
            def _():
                line_copy(high, ch, -1).start()

            pair_copy(high, ch).start()

    early = CHUNKS // 2
    for ch in range(early):
        relay(0, ch)
    filter_parts(rounds[0])
    send_parts(rounds[1])
    for ch in range(early, CHUNKS):
        relay(0, ch)
    await_filt(rounds[0])

    @pl.when(is_end)
    def _():
        for j in range(cap):
            far_filt_copy(j, inward).start()

    for ch in range(early):
        relay(1, ch)
    filter_parts(rounds[1])
    for ch in range(early, CHUNKS):
        relay(1, ch)

    def relay_step(s, _):
        for ch in range(CHUNKS):
            relay(s, ch)
        return 0

    lax.fori_loop(2, n_z - 2, relay_step, 0)

    for ch in range(CHUNKS):
        own_copy(ch).wait()

    def await_pair(src, _):
        @pl.when(holds(z, src))
        def _():
            for ch in range(CHUNKS):
                pair_arrival(src, ch).wait_recv()

        return 0

    lax.fori_loop(0, n_z, await_pair, 0)

    def product(values, slot, rows, factors):
        return lax.dot_general(
            values[slot, rows, :], factors, (((1,), (1,)), ((), ())),
            preferred_element_type=jnp.float32,
        )

    def place_of(slot):
        start = lax.rem(slot * depth, span)
        owner = start // share
        return owner, pl.ds(pl.multiple_of(start - owner * share, depth), depth)

    @pl.when(is_helper)
    def _():
        base = jnp.where(z == 1, half, 0) * 2
        for j in range(cap):
            cols = slice(j * BLK, (j + 1) * BLK)
            far_filt_copy(j, -inward).wait_recv()
            for ch in range(CHUNKS):
                rows = pl.ds(ch * rc, rc)
                value = jnp.zeros((rc, BLK), jnp.float32)
                for i in range(2 * half):
                    owner, inner = place_of(base + i)
                    value += product(v_all, base + i, rows, far_filt[owner, cols, inner])
                far_out[j, rows, :] = value.astype(jnp.bfloat16)
                far_copy(j, ch, -inward).start()

    def add_round(r):
        def step(i, _):
            slot = r * half * 2 + i
            owner, inner = place_of(slot)
            for ch in range(CHUNKS):
                rows = pl.ds(ch * rc, rc)
                acc[rows, :] += product(v_all, slot, rows, filt[r, owner, :, inner])
            return 0

        lax.fori_loop(0, 2 * half, step, 0)

    acc[...] = jnp.zeros_like(acc)

    @pl.when(jnp.logical_not(is_end))
    def _():
        add_round(rounds[0])

    await_filt(rounds[1])
    add_round(rounds[1])
    x_copy.wait()

    def expand(values):
        return [
            sum(pick[j][i] * values[:, j * BLK : (j + 1) * BLK] for j in range(cap))
            for i in range(blocks)
        ]

    def finish(ch):
        rows = slice(ch * rc, (ch + 1) * rc)

        @pl.when(is_end)
        def _():
            for j in range(cap):
                cols = slice(j * BLK, (j + 1) * BLK)
                far_copy(j, ch, inward).wait_recv()
                acc[rows, cols] += far_in[j, rows, :].astype(jnp.float32)

        weights = acc[rows, :].astype(jnp.bfloat16)
        for i, block in enumerate(expand(weights.astype(jnp.float32))):
            w_ref[rows, i * BLK : (i + 1) * BLK] = block.astype(jnp.bfloat16)
        value = jnp.dot(x_buf[:, rows], weights, preferred_element_type=jnp.float32)
        if ch == 0:
            pred_acc[...] = value
        else:
            pred_acc[...] += value

    for ch in range(CHUNKS):
        finish(ch)

    for d in range(1, n_t):
        to = peer(d)
        mine = pl.ds(pl.multiple_of(to * test_rows, test_rows), test_rows)
        pred_out[to] = pred_acc[mine, :].astype(jnp.bfloat16)
        pred_copy(to, t).start()
    for d in range(1, n_t):
        pred_copy(peer(d), peer(d)).wait_recv()
    total = pred_acc[pl.ds(pl.multiple_of(t * test_rows, test_rows), test_rows), :]
    for d in range(1, n_t):
        total = total + pred_in[peer(d)].astype(jnp.float32)
    for i, block in enumerate(expand(total)):
        pred_ref[:, i * BLK : (i + 1) * BLK] = block.astype(jnp.bfloat16)

    for d in range(1, n_t):
        for r in rounds:
            part_copy(r, peer(d), t).wait_send()
            filt_copy(r, peer(d), t).wait_send()
        pred_copy(peer(d), t).wait_send()

    @pl.when(is_end)
    def _():
        for j in range(cap):
            far_filt_copy(j, inward).wait_send()

    @pl.when(is_helper)
    def _():
        for j in range(cap):
            for ch in range(CHUNKS):
                far_copy(j, ch, -inward).wait_send()

    def drain(src, _):
        for ch in range(CHUNKS):

            @pl.when(holds(z, src))
            def _():
                pair_copy(src, ch).wait_send()

            @pl.when((src <= z) & (z < n_z - 1) & holds(z, src) & holds(z + 1, src))
            def _():
                line_copy(src, ch, 1).wait_send()

            @pl.when((src >= z) & (z > 0) & holds(z, src) & holds(z - 1, src))
            def _():
                line_copy(src, ch, -1).wait_send()

        return 0

    lax.fori_loop(0, n_z, drain, 0)


def body(n_t, n_v, u_train, y_train, sing, lambdas, lam_index, live, v_basis, x_test):
    time_rows, features = u_train.shape
    columns = y_train.shape[1]
    blocks = lam_index.shape[0]
    cap = blocks - blocks // 3
    used = cap * BLK
    rows_v, depth = v_basis.shape
    tests = x_test.shape[0]
    share = features // n_t // 2
    n_z = n_v // 2
    low, full = jnp.bfloat16, jnp.float32
    smem = pl.BlockSpec(memory_space=pltpu.SMEM)
    vmem = pl.BlockSpec(memory_space=pltpu.VMEM)
    anywhere = pl.BlockSpec(memory_space=pl.ANY)
    dma = pltpu.SemaphoreType.DMA
    return pl.pallas_call(
        functools.partial(kernel, n_t, n_v, cap),
        out_shape=(
            jax.ShapeDtypeStruct((rows_v, columns), low),
            jax.ShapeDtypeStruct((tests // n_t, columns), low),
        ),
        in_specs=[smem, smem, smem, vmem, vmem, anywhere, anywhere, anywhere],
        out_specs=(vmem, vmem),
        scratch_shapes=[
            pltpu.VMEM((time_rows, features), low),
            pltpu.VMEM((tests, rows_v), low),
            pltpu.VMEM((n_v, rows_v, depth), low),
            pltpu.VMEM((2, n_t, used, share), low),
            pltpu.VMEM((2, n_t, used, share), low),
            pltpu.VMEM((2, used, share), full),
            pltpu.VMEM((2, n_t, used, share), low),
            pltpu.VMEM((rows_v, used), full),
            pltpu.VMEM((tests, used), full),
            pltpu.VMEM((n_t, tests // n_t, used), low),
            pltpu.VMEM((n_t, tests // n_t, used), low),
            dma((2, n_t)),
            dma,
            dma((CHUNKS,)),
            dma((n_z, CHUNKS)),
            dma((n_z, CHUNKS)),
            dma((n_z, CHUNKS)),
            dma((n_z, CHUNKS)),
            dma((n_z, CHUNKS)),
            dma((2, n_t)),
            dma((2, n_t)),
            dma((2, n_t)),
            dma((2, n_t)),
            dma((n_t,)),
            dma((n_t,)),
            pltpu.VMEM((n_t, used, share), low),
            pltpu.VMEM((cap, rows_v, BLK), low),
            pltpu.VMEM((cap, rows_v, BLK), low),
            dma((cap,)),
            dma((cap,)),
            dma((cap, CHUNKS)),
            dma((cap, CHUNKS)),
        ],
        compiler_params=pltpu.CompilerParams(collective_id=0, has_side_effects=True),
    )(live, lam_index, lambdas, sing.reshape(1, features), y_train, u_train, v_basis, x_test)


def solution(mesh):
    placed = (
        P("tm", None),
        P("tm", "vox"),
        P(),
        P(),
        P("vox"),
        P("vox"),
        P("tm", "vox"),
        P(None, "tm"),
    )
    return jax.shard_map(
        functools.partial(body, mesh.shape["tm"], mesh.shape["vox"]),
        mesh=mesh,
        in_specs=placed,
        out_specs=(P("tm", "vox"), P("tm", "vox")),
        check_vma=False,
    )
```

```python
import functools

import jax
import jax.numpy as jnp
from jax import lax
from jax.experimental import pallas as pl
from jax.experimental.pallas import tpu as pltpu
from jax.sharding import PartitionSpec as P

BLK = 128
CHUNKS = 4
TILE = 256
MESH = pl.DeviceIdType.MESH


def one_hot(live_ref, cap):
    blocks = live_ref.shape[0]
    live = [live_ref[i] for i in range(blocks)]
    before = [sum(live[:i], jnp.int32(0)) for i in range(blocks)]
    return [
        [jnp.where(before[i] == j, live[i], 0).astype(jnp.float32) for i in range(blocks)]
        for j in range(cap)
    ]


def expand(cap, live_ref, w_in, pred_in, w_ref, pred_ref):
    pick = one_hot(live_ref, cap)
    for source, target in ((w_in, w_ref), (pred_in, pred_ref)):
        values = [source[:, j * BLK : (j + 1) * BLK].astype(jnp.float32) for j in range(cap)]
        for i in range(live_ref.shape[0]):
            block = sum(pick[j][i] * values[j] for j in range(cap))
            target[:, i * BLK : (i + 1) * BLK] = block.astype(target.dtype)


def kernel(
    n_t,
    n_v,
    cap,
    live_ref,
    index_ref,
    lambda_ref,
    sing_ref,
    y_ref,
    u_ref,
    v_ref,
    x_ref,
    w_ref,
    pred_ref,
    u_buf,
    x_buf,
    v_all,
    part_out,
    part_in,
    part_own,
    filt,
    acc,
    pred_acc,
    pred_out,
    pred_in,
    u_sem,
    x_sem,
    own_sem,
    right_sem,
    left_sem,
    line_sem,
    pair_send,
    pair_recv,
    rs_send,
    rs_recv,
    ag_send,
    ag_recv,
    q_send,
    q_recv,
    far_filt,
    far_out,
    far_in,
    far_filt_send,
    far_filt_recv,
    far_send,
    far_recv,
    hand_send,
    hand_recv,
):
    t = lax.axis_index("tm")
    v = lax.axis_index("vox")
    n_z = n_v // 2
    z, core = v // 2, v % 2
    mate = z * 2 + 1 - core
    rows_v, depth = v_ref.shape
    blocks = live_ref.shape[0]
    share = part_own.shape[2]
    half = n_z // 2
    span = n_t * share
    first_round = jnp.where(z < half, 1, 0)
    at_low, at_high = z == 0, z == n_z - 1
    is_end = at_low | at_high
    is_helper = (z == 1) | (z == n_z - 2)

    def holds(zz, src):
        return jnp.logical_not(
            ((zz == 0) & (src >= half)) | ((zz == n_z - 1) & (src < half))
        )
    test_rows = pred_out.shape[1]
    rc = rows_v // CHUNKS

    def u_copy(r, owner):
        cols = pl.ds(pl.multiple_of(r * span + owner * share, share), share)
        return pltpu.make_async_copy(u_ref.at[:, cols], u_buf.at[:, cols], u_sem.at[r, owner])

    def own_copy(ch):
        rows = pl.ds(ch * rc, rc)
        return pltpu.make_async_copy(v_ref.at[rows], v_all.at[v, rows], own_sem.at[ch])

    def line_copy(src, ch, step, first=False):
        rows = pl.ds(ch * rc, rc)
        slot = src * 2 + core
        return pltpu.make_async_remote_copy(
            src_ref=v_ref.at[rows] if first else v_all.at[slot, rows],
            dst_ref=v_all.at[slot, rows],
            send_sem=(right_sem if step > 0 else left_sem).at[src, ch],
            recv_sem=line_sem.at[src, ch],
            device_id={"vox": v + 2 * step},
            device_id_type=MESH,
        )

    def pair_copy(src, ch, first=False):
        rows = pl.ds(ch * rc, rc)
        slot = src * 2 + core
        return pltpu.make_async_remote_copy(
            src_ref=v_ref.at[rows] if first else v_all.at[slot, rows],
            dst_ref=v_all.at[slot, rows],
            send_sem=pair_send.at[src, ch],
            recv_sem=pair_recv.at[src, ch],
            device_id={"vox": mate},
            device_id_type=MESH,
        )

    def pair_arrival(src, ch):
        rows = pl.ds(ch * rc, rc)
        slot = src * 2 + 1 - core
        return pltpu.make_async_remote_copy(
            src_ref=v_all.at[slot, rows],
            dst_ref=v_all.at[slot, rows],
            send_sem=pair_send.at[src, ch],
            recv_sem=pair_recv.at[src, ch],
            device_id={"vox": mate},
            device_id_type=MESH,
        )

    def peer(d):
        return lax.rem(t + d, n_t)

    def part_copy(r, to, owner):
        return pltpu.make_async_remote_copy(
            src_ref=part_out.at[r, to],
            dst_ref=part_in.at[r, owner],
            send_sem=rs_send.at[r, to],
            recv_sem=rs_recv.at[r, owner],
            device_id={"tm": to},
            device_id_type=MESH,
        )

    def filt_copy(r, to, owner):
        return pltpu.make_async_remote_copy(
            src_ref=filt.at[r, owner],
            dst_ref=filt.at[r, owner],
            send_sem=ag_send.at[r, to],
            recv_sem=ag_recv.at[r, owner],
            device_id={"tm": to},
            device_id_type=MESH,
        )

    relayed = n_t == 4
    near = [t + 1 - 2 * lax.rem(t, 2), lax.rem(t + 2, n_t)] if relayed else [peer(d) for d in range(1, n_t)]

    def relay_copy(r, k, to, owner):
        rows = pl.ds(k * (filt.shape[2] // 2), filt.shape[2] // 2)
        return pltpu.make_async_remote_copy(
            src_ref=filt.at[r, owner, rows],
            dst_ref=filt.at[r, owner, rows],
            send_sem=hand_send.at[r, k],
            recv_sem=hand_recv.at[r, k],
            device_id={"tm": to},
            device_id_type=MESH,
        )

    def pred_copy(to, owner):
        return pltpu.make_async_remote_copy(
            src_ref=pred_out.at[to],
            dst_ref=pred_in.at[owner],
            send_sem=q_send.at[to],
            recv_sem=q_recv.at[owner],
            device_id={"tm": to},
            device_id_type=MESH,
        )

    inward = jnp.where(z < half, 1, -1)

    def far_filt_copy(j, step):
        rows = pl.ds(j * BLK, BLK)
        return pltpu.make_async_remote_copy(
            src_ref=filt.at[first_round, :, rows, :],
            dst_ref=far_filt.at[:, rows, :],
            send_sem=far_filt_send.at[j],
            recv_sem=far_filt_recv.at[j],
            device_id={"vox": v + 2 * step},
            device_id_type=MESH,
        )

    def far_copy(j, ch, step):
        rows = pl.ds(ch * rc, rc)
        return pltpu.make_async_remote_copy(
            src_ref=far_out.at[j, rows],
            dst_ref=far_in.at[j, rows],
            send_sem=far_send.at[j, ch],
            recv_sem=far_recv.at[j, ch],
            device_id={"vox": v + 2 * step},
            device_id_type=MESH,
        )

    rounds = (first_round, 1 - first_round)
    for r in rounds:
        for d in range(n_t):
            u_copy(r, peer((d + 1) % n_t)).start()

    barrier = pltpu.get_barrier_semaphore()
    for d in range(1, n_t):
        pl.semaphore_signal(barrier, inc=1, device_id={"tm": peer(d)}, device_id_type=MESH)
    pl.semaphore_signal(barrier, inc=1, device_id={"vox": mate}, device_id_type=MESH)

    @pl.when(z > 0)
    def _():
        pl.semaphore_signal(barrier, inc=1, device_id={"vox": v - 2}, device_id_type=MESH)

    @pl.when(z < n_z - 1)
    def _():
        pl.semaphore_signal(barrier, inc=1, device_id={"vox": v + 2}, device_id_type=MESH)

    neighbours = jnp.where(z > 0, 1, 0) + jnp.where(z < n_z - 1, 1, 0)
    pl.semaphore_wait(barrier, n_t + neighbours)

    for ch in range(CHUNKS):

        @pl.when(z > 0)
        def _():
            line_copy(z, ch, -1, True).start()

        @pl.when(z < n_z - 1)
        def _():
            line_copy(z, ch, 1, True).start()

    pick = one_hot(live_ref, cap)
    lam = [lambda_ref[index_ref[i]] for i in range(blocks)]
    slot_lam = [sum(pick[j][i] * lam[i] for i in range(blocks)) for j in range(cap)]
    slot_live = [sum(pick[j][i] for i in range(blocks)) for j in range(cap)]

    y_cols = [y_ref[:, i * BLK : (i + 1) * BLK].astype(jnp.float32) for i in range(blocks)]
    y_t = jnp.concatenate(
        [sum(pick[j][i] * y_cols[i] for i in range(blocks)).T for j in range(cap)], axis=0
    ).astype(jnp.bfloat16)

    def make_parts(r, send):
        for d in range(1, n_t + 1):
            to = peer(d % n_t)
            u_copy(r, to).wait()

            def tile(i, _, to=to, d=d):
                off = pl.multiple_of(i * TILE, TILE)
                cols = pl.ds(pl.multiple_of(r * span + to * share + i * TILE, TILE), TILE)
                value = jnp.dot(y_t, u_buf[:, cols], preferred_element_type=jnp.float32)
                if d < n_t:
                    part_out[r, to, :, pl.ds(off, TILE)] = value.astype(jnp.bfloat16)
                else:
                    part_own[r, :, pl.ds(off, TILE)] = value
                return 0

            lax.fori_loop(0, share // TILE, tile, 0)
            if send and d < n_t:
                part_copy(r, to, t).start()

    def send_parts(r):
        for d in range(1, n_t):
            part_copy(r, peer(d), t).start()

    def filter_parts(r):
        for d in range(1, n_t):
            part_copy(r, peer(d), peer(d)).wait_recv()
        for i in range(share // TILE):
            cols = slice(i * TILE, (i + 1) * TILE)
            place = pl.multiple_of(r * span + t * share + i * TILE, TILE)
            sing = sing_ref[:, pl.ds(place, TILE)]
            for j in range(cap):
                rows = slice(j * BLK, (j + 1) * BLK)
                total = part_own[r, rows, cols]
                for d in range(1, n_t):
                    total = total + part_in[r, peer(d), rows, cols].astype(jnp.float32)
                factor = sing / (sing * sing + slot_lam[j]) * slot_live[j]
                filt[r, t, rows, cols] = (total * factor).astype(jnp.bfloat16)
        for to in near:
            filt_copy(r, to, t).start()

    def forward_filt(r):
        for to in near:
            filt_copy(r, to, to).wait_recv()
        if relayed:
            for k in range(2):
                relay_copy(r, k, near[k], near[1 - k]).start()

    def await_filt(r):
        if relayed:
            for k in range(2):
                relay_copy(r, k, near[k], n_t - 1 - t).wait_recv()

    make_parts(rounds[0], True)

    for ch in range(CHUNKS):
        pair_copy(z, ch, True).start()
        own_copy(ch).start()
    x_copy = pltpu.make_async_copy(x_ref, x_buf, x_sem)
    x_copy.start()

    make_parts(rounds[1], False)

    def relay(s, ch):
        low, high = z - 1 - s, z + 1 + s

        @pl.when((low >= 0) & holds(z, low))
        def _():
            line_copy(low, ch, -1).wait_recv()

            @pl.when((z < n_z - 1) & holds(z + 1, low))
            def _():
                line_copy(low, ch, 1).start()

            pair_copy(low, ch).start()

        @pl.when((high < n_z) & holds(z, high))
        def _():
            line_copy(high, ch, 1).wait_recv()

            @pl.when((z > 0) & holds(z - 1, high))
            def _():
                line_copy(high, ch, -1).start()

            pair_copy(high, ch).start()

    def product(values, slot, rows, factors):
        return lax.dot_general(
            values[slot, rows, :], factors, (((1,), (1,)), ((), ())),
            preferred_element_type=jnp.float32,
        )

    def place_of(slot):
        start = lax.rem(slot * depth, span)
        owner = start // share
        return owner, pl.ds(pl.multiple_of(start - owner * share, depth), depth)

    base = jnp.where(z == 1, half, 0) * 2

    def settle(ch):
        own_copy(ch).wait()

        def step(src, _):
            @pl.when(holds(z, src))
            def _():
                pair_arrival(src, ch).wait_recv()

            return 0

        lax.fori_loop(0, n_z, step, 0)

    def add_round(r, ch):
        rows = pl.ds(ch * rc, rc)

        def step(i, value):
            slot = r * half * 2 + i
            owner, inner = place_of(slot)
            return value + product(v_all, slot, rows, filt[r, owner, :, inner])

        value = jnp.zeros((rc, acc.shape[1]), jnp.float32)
        for i in range(2 * half):
            value = step(i, value)
        return value

    def far_half(ch):
        rows = pl.ds(ch * rc, rc)

        @pl.when(jnp.logical_not(is_end))
        def _():
            acc[rows, :] = add_round(rounds[0], ch)

        @pl.when(is_end)
        def _():
            acc[rows, :] = jnp.zeros((rc, acc.shape[1]), jnp.float32)

    def help_end(j, chunks):
        cols = slice(j * BLK, (j + 1) * BLK)

        @pl.when(is_helper)
        def _():
            if chunks[0] == 0:
                far_filt_copy(j, -inward).wait_recv()
            for ch in chunks:
                rows = pl.ds(ch * rc, rc)
                value = jnp.zeros((rc, BLK), jnp.float32)
                for i in range(2 * half):
                    owner, inner = place_of(base + i)
                    value += product(v_all, base + i, rows, far_filt[owner, cols, inner])
                far_out[j, rows, :] = value.astype(jnp.bfloat16)
                far_copy(j, ch, -inward).start()

    early, last = CHUNKS // 2, CHUNKS - 1
    for ch in range(early):
        relay(0, ch)
    filter_parts(rounds[0])
    for ch in range(early, last):
        relay(0, ch)
    forward_filt(rounds[0])
    send_parts(rounds[1])
    relay(0, last)
    await_filt(rounds[0])

    @pl.when(is_end)
    def _():
        for j in range(cap):
            far_filt_copy(j, inward).start()

    def relay_step(s, _):
        for ch in range(CHUNKS):
            relay(s, ch)
        return 0

    lax.fori_loop(1, n_z - 3, relay_step, 0)
    for ch in range(early):
        relay(n_z - 3, ch)
    filter_parts(rounds[1])
    for ch in range(early, last):
        relay(n_z - 3, ch)
    for ch in range(early):
        settle(ch)
        far_half(ch)
    forward_filt(rounds[1])
    for ch in range(early, last):
        settle(ch)
        far_half(ch)
    help_end(0, list(range(last)))
    relay(n_z - 3, last)
    settle(last)
    help_end(0, [last])
    far_half(last)
    help_end(1, list(range(CHUNKS)))
    for j in range(2, cap):
        help_end(j, list(range(CHUNKS)))
    await_filt(rounds[1])
    x_copy.wait()

    def finish(ch):
        rows = slice(ch * rc, (ch + 1) * rc)
        acc[rows, :] += add_round(rounds[1], ch)

        @pl.when(is_end)
        def _():
            for j in range(cap):
                cols = slice(j * BLK, (j + 1) * BLK)
                far_copy(j, ch, inward).wait_recv()
                acc[rows, cols] += far_in[j, rows, :].astype(jnp.float32)

        weights = acc[rows, :].astype(jnp.bfloat16)
        w_ref[rows, :] = weights
        value = jnp.dot(x_buf[:, rows], weights, preferred_element_type=jnp.float32)
        if ch == 0:
            pred_acc[...] = value
        else:
            pred_acc[...] += value

    for ch in range(CHUNKS):
        finish(ch)

    for d in range(1, n_t):
        to = peer(d)
        mine = pl.ds(pl.multiple_of(to * test_rows, test_rows), test_rows)
        pred_out[to] = pred_acc[mine, :].astype(jnp.bfloat16)
        pred_copy(to, t).start()
    for d in range(1, n_t):
        pred_copy(peer(d), peer(d)).wait_recv()
    total = pred_acc[pl.ds(pl.multiple_of(t * test_rows, test_rows), test_rows), :]
    for d in range(1, n_t):
        total = total + pred_in[peer(d)].astype(jnp.float32)
    pred_ref[...] = total.astype(jnp.bfloat16)

    for d in range(1, n_t):
        for r in rounds:
            part_copy(r, peer(d), t).wait_send()
        pred_copy(peer(d), t).wait_send()
    for r in rounds:
        for to in near:
            filt_copy(r, to, t).wait_send()
        if relayed:
            for k in range(2):
                relay_copy(r, k, near[k], near[1 - k]).wait_send()

    @pl.when(is_end)
    def _():
        for j in range(cap):
            far_filt_copy(j, inward).wait_send()

    @pl.when(is_helper)
    def _():
        for j in range(cap):
            for ch in range(CHUNKS):
                far_copy(j, ch, -inward).wait_send()

    def drain(src, _):
        for ch in range(CHUNKS):

            @pl.when(holds(z, src))
            def _():
                pair_copy(src, ch).wait_send()

            @pl.when((src <= z) & (z < n_z - 1) & holds(z, src) & holds(z + 1, src))
            def _():
                line_copy(src, ch, 1).wait_send()

            @pl.when((src >= z) & (z > 0) & holds(z, src) & holds(z - 1, src))
            def _():
                line_copy(src, ch, -1).wait_send()

        return 0

    lax.fori_loop(0, n_z, drain, 0)


def body(n_t, n_v, u_train, y_train, sing, lambdas, lam_index, live, v_basis, x_test):
    time_rows, features = u_train.shape
    columns = y_train.shape[1]
    blocks = lam_index.shape[0]
    cap = blocks - blocks // 3
    used = cap * BLK
    rows_v, depth = v_basis.shape
    tests = x_test.shape[0]
    share = features // n_t // 2
    n_z = n_v // 2
    low, full = jnp.bfloat16, jnp.float32
    smem = pl.BlockSpec(memory_space=pltpu.SMEM)
    vmem = pl.BlockSpec(memory_space=pltpu.VMEM)
    anywhere = pl.BlockSpec(memory_space=pl.ANY)
    dma = pltpu.SemaphoreType.DMA
    weights, predicted = pl.pallas_call(
        functools.partial(kernel, n_t, n_v, cap),
        out_shape=(
            jax.ShapeDtypeStruct((rows_v, used), low),
            jax.ShapeDtypeStruct((tests // n_t, used), low),
        ),
        in_specs=[smem, smem, smem, vmem, vmem, anywhere, anywhere, anywhere],
        out_specs=(vmem, vmem),
        scratch_shapes=[
            pltpu.VMEM((time_rows, features), low),
            pltpu.VMEM((tests, rows_v), low),
            pltpu.VMEM((n_v, rows_v, depth), low),
            pltpu.VMEM((2, n_t, used, share), low),
            pltpu.VMEM((2, n_t, used, share), low),
            pltpu.VMEM((2, used, share), full),
            pltpu.VMEM((2, n_t, used, share), low),
            pltpu.VMEM((rows_v, used), full),
            pltpu.VMEM((tests, used), full),
            pltpu.VMEM((n_t, tests // n_t, used), low),
            pltpu.VMEM((n_t, tests // n_t, used), low),
            dma((2, n_t)),
            dma,
            dma((CHUNKS,)),
            dma((n_z, CHUNKS)),
            dma((n_z, CHUNKS)),
            dma((n_z, CHUNKS)),
            dma((n_z, CHUNKS)),
            dma((n_z, CHUNKS)),
            dma((2, n_t)),
            dma((2, n_t)),
            dma((2, n_t)),
            dma((2, n_t)),
            dma((n_t,)),
            dma((n_t,)),
            pltpu.VMEM((n_t, used, share), low),
            pltpu.VMEM((cap, rows_v, BLK), low),
            pltpu.VMEM((cap, rows_v, BLK), low),
            dma((cap,)),
            dma((cap,)),
            dma((cap, CHUNKS)),
            dma((cap, CHUNKS)),
            dma((2, 2)),
            dma((2, 2)),
        ],
        compiler_params=pltpu.CompilerParams(collective_id=0, has_side_effects=True),
    )(live, lam_index, lambdas, sing.reshape(1, features), y_train, u_train, v_basis, x_test)
    return pl.pallas_call(
        functools.partial(expand, cap),
        out_shape=(
            jax.ShapeDtypeStruct((rows_v, columns), low),
            jax.ShapeDtypeStruct((tests // n_t, columns), low),
        ),
        in_specs=[smem, vmem, vmem],
        out_specs=(vmem, vmem),
    )(live, weights, predicted)


def solution(mesh):
    placed = (
        P("tm", None),
        P("tm", "vox"),
        P(),
        P(),
        P("vox"),
        P("vox"),
        P("tm", "vox"),
        P(None, "tm"),
    )
    return jax.shard_map(
        functools.partial(body, mesh.shape["tm"], mesh.shape["vox"]),
        mesh=mesh,
        in_specs=placed,
        out_specs=(P("tm", "vox"), P("tm", "vox")),
        check_vma=False,
    )
```
